256 devices in a mesh: azim: 32 (over y_hi, z, core), beam: 2 (over y_lo), sweep: 4 (over x).
Axes of the slice: x: 4, y: 4 (y_hi: 2, y_lo: 2; y = y_hi * 2 + y_lo), z: 8, core: 2. Of those that a mesh axis runs over, the one named last changes fastest.
Arguments:
- features: bfloat16 [2048, 4, 4, 256], P('azim', 'sweep', 'beam'), may hold values from -16 to 16
- cotangent: bfloat16 [2048, 4, 4, 256], P('azim', 'sweep', 'beam'), may hold values from -6 to 6
- w_query: bfloat16 [256, 256], replicated
- w_key: bfloat16 [256, 256], replicated
- w_value: bfloat16 [256, 256], replicated, may hold values from -0.375 to 0.375
- w_out: bfloat16 [256, 256], replicated, may hold values from -0.375 to 0.375
- w_conv: bfloat16 [256, 27, 256], replicated, may hold values from -0.078125 to 0.078125
- sector_mask: int32 [32, 32], replicated, may hold values from 0 to 1, as said below
Outputs:
- features_grad: bfloat16 [2048, 4, 4, 256], P('azim', 'sweep', 'beam')
- weight_grads: float32 [256, 31, 256], P('azim', None, ('beam', 'sweep'))
The draws below stay inside these ranges and needn't reach their ends.
Inputs may be any that keep to these rules, and one draw needn't show every extreme that they name: `sector_mask`: entry [i, j] is 1 where query sector i may attend to key sector j, else 0; every diagonal entry is 1.
All inputs are finite; a program needn't handle non-finite values.
Results may differ from the reference program's by a relative error of at most 0.012.
The reference program's roundings to bfloat16 on the way count: a program that leaves them out, or rounds other values in their place, can miss the bound.
Values may be sent and summed in bfloat16 or wider, within the bound.
A program may use at most 128 MiB of HBM per device.

```python
import jax
import jax.numpy as jnp
from jax import lax

D = 256
HEADS = 8
SECTOR = 64
TAPS = 27
NAZ = 2048
NSW = 4
NBM = 4
SECTORS = 32


def draw_features(key, part):
    extent = (NAZ, NSW, NBM, D)
    subkeys = jax.random.split(key, 1)
    return jnp.clip(jax.random.normal(subkeys[0], extent, jnp.float32), -6.0, 6.0).astype(jnp.bfloat16)


def projection_pair(key):
    first_key, second_key = jax.random.split(jax.random.fold_in(key, 11))
    spread = D ** (-0.5)
    query_part = jnp.clip(jax.random.normal(first_key, (D, D), jnp.float32), -3.0, 3.0) * spread
    other_part = jnp.clip(jax.random.normal(second_key, (D, D), jnp.float32), -3.0, 3.0) * spread
    return (query_part, other_part)


def draw_w_query(key, part):
    return projection_pair(key)[0].astype(jnp.bfloat16)


def draw_w_key(key, part):
    return projection_pair(key)[1].astype(jnp.bfloat16)


def draw_sector_mask(key, part):
    first_key, second_key = jax.random.split(jax.random.fold_in(key, 23))
    row_rates = jax.random.randint(first_key, (SECTORS, 1), 15, 90)
    dice_rolls = jax.random.randint(second_key, (SECTORS, SECTORS), 0, 100)
    diagonal = jnp.arange(SECTORS)[:, None] == jnp.arange(SECTORS)[None, :]
    return jnp.where(diagonal, 1, (dice_rolls < row_rates).astype(jnp.int32)).astype(jnp.int32)


def level_of(own_key, dims, cuts, low, largest):
    loudness = 1.0
    for position, parts in cuts:
        heights = jax.random.uniform(jax.random.fold_in(jax.random.fold_in(own_key, 6), position), (parts,), jnp.float32, low / len(cuts), largest / len(cuts))
        loudness = loudness * jnp.repeat(jnp.exp(heights), dims[position] // parts).reshape((-1,) + (1,) * (len(dims) - 1 - position))
    return loudness


def centred(rng, dims, width, reach, pieces=(), kind=jnp.bfloat16):
    level = level_of(rng, dims, pieces, -0.22, 0.18) if pieces else 1.0
    array = jax.random.normal(rng, dims, jnp.float32) * width * level
    return jnp.minimum(jnp.maximum(array, -reach), reach).astype(kind)


def setup_inputs(seed: int = 0) -> dict:
    splits = jax.random.split(jax.random.key(seed), 9)
    return {
        "features": draw_features(jax.random.fold_in(splits[8], 71), 0),
        "cotangent": centred(splits[1], (NAZ, NSW, NBM, D), 1.0, 6.0, ((0, 32), (1, 4), (2, 2))),
        "w_query": draw_w_query(jax.random.fold_in(splits[8], 71), 0),
        "w_key": draw_w_key(jax.random.fold_in(splits[8], 71), 0),
        "w_value": centred(splits[4], (D, D), D ** -0.5, 0.375),
        "w_out": centred(splits[5], (D, D), D ** -0.5, 0.375),
        "w_conv": centred(splits[6], (D, TAPS, D), (TAPS * D) ** -0.5, 0.078125),
        "sector_mask": draw_sector_mask(jax.random.fold_in(splits[8], 71), 0),
    }


highest = lax.Precision.HIGHEST
masked_score = -1e30


def matmul(left_side, right_side):
    return jnp.dot(left_side.astype(jnp.float32), right_side.astype(jnp.float32), precision=highest)


def rounded(tensor):
    return lax.optimization_barrier(tensor.astype(jnp.bfloat16)).astype(jnp.float32)


def pad_grid(grid_in):
    wrapped = jnp.concatenate([grid_in[-1:], grid_in, grid_in[:1]], axis=0)
    return jnp.pad(wrapped, ((0, 0), (1, 1), (1, 1), (0, 0)))


def reference(features, cotangent, w_query, w_key, w_value, w_out, w_conv, sector_mask):
    extent = features.shape
    col_count, sweeps, beam_rows, channels = extent
    tokens = col_count * sweeps * beam_rows
    sequences = sweeps * beam_rows
    head_size = channels // HEADS
    score_scale = head_size ** -0.5
    flat_in = features.astype(jnp.float32).reshape(tokens, channels)
    queries = rounded(matmul(flat_in, w_query))
    key_proj = rounded(matmul(flat_in, w_key))
    values = rounded(matmul(flat_in, w_value))
    allowed = jnp.repeat(jnp.repeat(sector_mask, SECTOR, axis=0), SECTOR, axis=1) > 0

    def by_sequence(tensor):
        return tensor.reshape(col_count, sequences, HEADS, head_size).transpose(1, 0, 2, 3)

    def by_token(tensor):
        return tensor.transpose(1, 0, 2, 3).reshape(tokens, channels)

    def scores_of(query_seq, key_seq):
        raw_scores = jnp.einsum("ahe,khe->hak", query_seq, key_seq, precision=highest)
        return jnp.where(allowed, raw_scores * score_scale, masked_score)

    def forward_one(operands):
        query_seq, key_seq, value_seq = operands
        scores = scores_of(query_seq, key_seq)
        peak_score = jnp.max(scores, axis=-1)
        logsum = peak_score + jnp.log(jnp.sum(jnp.exp(scores - peak_score[..., None]), axis=-1))
        weights_full = jnp.where(allowed, jnp.exp(scores - logsum[..., None]), 0.0)
        attended_one = rounded(jnp.einsum("hak,khe->ahe", rounded(weights_full), value_seq, precision=highest))
        return attended_one, logsum

    attended_seq, logsum_seq = lax.map(forward_one, (by_sequence(queries), by_sequence(key_proj), by_sequence(values)))
    attended = by_token(attended_seq)
    layer_out = rounded(flat_in + matmul(attended, w_out))
    layer_pad = pad_grid(layer_out.reshape(extent).astype(jnp.bfloat16))
    cot_pad = pad_grid(cotangent)
    cot_flat = cotangent.astype(jnp.float32).reshape(tokens, channels)
    grad_layer = cot_flat
    conv_grads = []
    for offset_one in (-1, 0, 1):
        for offset_two in (-1, 0, 1):
            for offset_three in (-1, 0, 1):
                tap_index = 9 * (offset_one + 1) + 3 * (offset_two + 1) + (offset_three + 1)
                cot_piece = cot_pad[1 - offset_one:1 - offset_one + col_count, 1 - offset_two:1 - offset_two + sweeps, 1 - offset_three:1 - offset_three + beam_rows]
                layer_piece = layer_pad[1 + offset_one:1 + offset_one + col_count, 1 + offset_two:1 + offset_two + sweeps, 1 + offset_three:1 + offset_three + beam_rows]
                grad_layer = grad_layer + matmul(cot_piece.reshape(tokens, channels), w_conv[:, tap_index, :].T)
                conv_grads.append(matmul(layer_piece.reshape(tokens, channels).T, cot_flat))
    grad_layer_bf = rounded(grad_layer)
    grad_attended = rounded(matmul(grad_layer_bf, w_out.T))

    def backward_one(operands):
        query_seq, key_seq, value_seq, attended_one, grad_one, logsum = operands
        scores = scores_of(query_seq, key_seq)
        weights_full = jnp.where(allowed, jnp.exp(scores - logsum[..., None]), 0.0)
        row_delta = jnp.einsum("ahe,ahe->ha", grad_one, attended_one, precision=highest)
        grad_prob = jnp.einsum("ahe,khe->hak", grad_one, value_seq, precision=highest)
        grad_score = rounded(weights_full * (grad_prob - row_delta[..., None]))
        grad_query_one = jnp.einsum("hak,khe->ahe", grad_score, key_seq, precision=highest) * score_scale
        grad_key_one = jnp.einsum("hak,ahe->khe", grad_score, query_seq, precision=highest) * score_scale
        grad_value_one = jnp.einsum("hak,ahe->khe", rounded(weights_full), grad_one, precision=highest)
        return grad_query_one, grad_key_one, grad_value_one

    grad_query_seq, grad_key_seq, grad_value_seq = lax.map(backward_one, (by_sequence(queries), by_sequence(key_proj), by_sequence(values), attended_seq, by_sequence(grad_attended), logsum_seq))
    grad_query = by_token(grad_query_seq)
    grad_key = by_token(grad_key_seq)
    grad_value = by_token(grad_value_seq)
    grad_in = grad_layer + matmul(grad_query, w_query.T) + matmul(grad_key, w_key.T) + matmul(grad_value, w_value.T)
    features_grad = grad_in.astype(jnp.bfloat16).reshape(extent)
    projection_grads = jnp.stack([matmul(flat_in.T, grad_query), matmul(flat_in.T, grad_key), matmul(flat_in.T, grad_value), matmul(attended.T, grad_layer_bf)], axis=1)
    weight_grads = jnp.concatenate([projection_grads, jnp.stack(conv_grads, axis=1)], axis=1)
    return features_grad, weight_grads
```

```python
import functools

import jax
import jax.numpy as jnp
from jax import lax
from jax.experimental import pallas as pl
from jax.experimental.pallas import tpu as pltpu
from jax.sharding import PartitionSpec as P

HEADS = 8
HEAD = 32
COLS = 64
RING = 32
CHIPS = 16
GROUP = 8
SWEEPS = 4
TAPS = 27
TILE = 256
SCALE = HEAD ** (-0.5)
MASKED = -1e30
MESH = pl.DeviceIdType.MESH
VMEM = pl.BlockSpec(memory_space=pltpu.VMEM)
F32 = jnp.float32
BF16 = jnp.bfloat16


def place():
    return lax.axis_index("azim"), lax.axis_index("beam"), lax.axis_index("sweep")


def member(azim, index):
    return (azim, lax.div(index, SWEEPS), lax.rem(index, SWEEPS))


def greet(devices):
    barrier = pltpu.get_barrier_semaphore()
    total = 0
    for first, last, device in devices:

        def one(i, carry, device=device):
            pl.semaphore_signal(barrier, inc=1, device_id=device(i), device_id_type=MESH)
            return carry

        lax.fori_loop(first, last, one, 0)
        total += last - first
    pl.semaphore_wait(barrier, total)


def remote(src, dst, send, recv, device):
    return pltpu.make_async_remote_copy(
        src_ref=src, dst_ref=dst, send_sem=send, recv_sem=recv, device_id=device, device_id_type=MESH
    )


def each(first, last, action):
    def step(i, carry):
        action(i)
        return carry

    lax.fori_loop(first, last, step, 0)


def halo_kernel(cot, edges, cot_all, low, high, send, recv, send_low, recv_low, send_high, recv_high):
    azim, beam, sweep = place()
    me = beam * SWEEPS + sweep
    after = lax.rem(azim + 1, RING)
    before = lax.rem(azim + RING - 1, RING)
    peer = lambda i: lax.rem(me + i, GROUP)
    greet(
        [
            (1, GROUP, lambda i: member(azim, peer(i))),
            (0, GROUP, lambda i: member(after, i)),
            (0, GROUP, lambda i: member(before, i)),
        ]
    )
    each(
        0,
        GROUP,
        lambda i: remote(
            edges.at[1], low.at[me], send_low.at[i], recv_low.at[me], member(after, i)
        ).start(),
    )
    each(
        0,
        GROUP,
        lambda i: remote(
            edges.at[0], high.at[me], send_high.at[i], recv_high.at[me], member(before, i)
        ).start(),
    )
    each(
        1,
        GROUP,
        lambda i: remote(
            cot, cot_all.at[me], send.at[peer(i)], recv.at[me], member(azim, peer(i))
        ).start(),
    )
    cot_all[pl.ds(me, 1)] = cot[...][None]
    each(
        1,
        GROUP,
        lambda i: remote(
            cot, cot_all.at[peer(i)], send.at[peer(i)], recv.at[peer(i)], member(azim, peer(i))
        ).wait(),
    )
    each(
        0,
        GROUP,
        lambda i: remote(
            edges.at[1], low.at[i], send_low.at[i], recv_low.at[i], member(after, i)
        ).wait(),
    )
    each(
        0,
        GROUP,
        lambda i: remote(
            edges.at[0], high.at[i], send_high.at[i], recv_high.at[i], member(before, i)
        ).wait(),
    )


def shifted(block, low, high):
    rows = lax.broadcasted_iota(jnp.int32, block.shape, 0)
    down = jnp.where(rows == 0, low, pltpu.roll(block, 1, 0))
    up = jnp.where(rows == COLS - 1, high, pltpu.roll(block, COLS - 1, 0))
    return up, block, down


def regroup():
    col = lax.broadcasted_iota(jnp.int32, (1, 1024), 1)
    source = ((col >> 5) & 3) * 256 + (col >> 7) * 32 + (col & 31)
    row = lax.broadcasted_iota(jnp.int32, (1024, 1024), 0)
    return jnp.where(row == source, 1.0, 0.0).astype(BF16)


def dot(left, right):
    return jnp.dot(left, right, preferred_element_type=F32)


def dot_nt(left, right):
    return lax.dot_general(left, right, (((1,), (1,)), ((), ())), preferred_element_type=F32)


def project_kernel(cot_all, low, high, feat, w_query, w_key, w_value, w_out, w_conv, grad_out, pack):
    _, beam, sweep = place()
    total = jnp.zeros((2 * COLS, 256), F32)
    for j in (-1, 0, 1):
        for k in (-1, 0, 1):
            ups, mids, downs = [], [], []
            for own in (0, 1):
                s_at = sweep - j
                b_at = beam * 2 + own - k
                inside = (s_at >= 0) & (s_at < SWEEPS) & (b_at >= 0) & (b_at < 4)
                s_at = jnp.clip(s_at, 0, SWEEPS - 1)
                pair_at = jnp.clip(beam + (own - k) // 2, 0, 1)
                index = pair_at * SWEEPS + s_at
                half = (own - k) % 2
                keep = jnp.where(inside, 1.0, 0.0)
                block = cot_all[index, half].astype(F32) * keep
                up, mid, down = shifted(
                    block,
                    low[index].astype(F32)[half : half + 1] * keep,
                    high[index].astype(F32)[half : half + 1] * keep,
                )
                ups.append(up)
                mids.append(mid)
                downs.append(down)
            for i, rows in ((-1, ups), (0, mids), (1, downs)):
                tap = 9 * (i + 1) + 3 * (j + 1) + (k + 1)
                rows = jnp.concatenate(rows, axis=0).astype(BF16)
                total += dot_nt(rows, w_conv[tap])
    me = beam * SWEEPS + sweep
    grad = cot_all[me].astype(F32).reshape(2 * COLS, 256) + total
    grad_out[...] = grad
    grad_att = dot_nt(grad.astype(BF16), w_out[...]).astype(BF16)
    rows = feat[...]
    queries = dot(rows, w_query[...]).astype(BF16)
    keys = dot(rows, w_key[...]).astype(BF16)
    values = dot(rows, w_value[...]).astype(BF16)
    wide = jnp.concatenate([keys, queries, grad_att, values], axis=1)
    packed = dot(wide, regroup()).astype(BF16)
    for b in (0, 1):
        for h in range(HEADS):
            pack[b * HEADS + h] = packed[b * COLS : (b + 1) * COLS, h * 128 : (h + 1) * 128]


def spread_kernel(pack, feat, same, other, feat_all, send, recv, send_f, recv_f, own_sem, pair_sem):
    azim, beam, sweep = place()
    me = beam * SWEEPS + sweep
    chip = lax.div(azim, 2)
    core = lax.rem(azim, 2)
    sibling = (2 * chip + 1 - core, beam, sweep)
    target = lambda i: lax.rem(chip + i, CHIPS)
    device = lambda q: (2 * q + core, beam, sweep)
    peer = lambda i: lax.rem(me + i, GROUP)
    greet(
        [
            (1, CHIPS, lambda i: device(target(i))),
            (0, 1, lambda i: sibling),
            (1, GROUP, lambda i: member(azim, peer(i))),
        ]
    )
    keep = pltpu.make_async_copy(pack.at[chip], same.at[chip], own_sem)
    keep.start()
    each(
        1,
        CHIPS,
        lambda i: remote(
            pack.at[target(i)], same.at[chip], send.at[target(i)], recv.at[chip], device(target(i))
        ).start(),
    )
    each(
        1,
        GROUP,
        lambda i: remote(
            feat, feat_all.at[me], send_f.at[peer(i)], recv_f.at[me], member(azim, peer(i))
        ).start(),
    )
    feat_all[pl.ds(me, 1)] = feat[...][None]
    keep.wait()
    each(
        1,
        CHIPS,
        lambda i: remote(
            pack.at[target(i)],
            same.at[target(i)],
            send.at[target(i)],
            recv.at[target(i)],
            device(target(i)),
        ).wait(),
    )
    relay = remote(same, other, pair_sem.at[0], pair_sem.at[1], sibling)
    relay.start()
    each(
        1,
        GROUP,
        lambda i: remote(
            feat, feat_all.at[peer(i)], send_f.at[peer(i)], recv_f.at[peer(i)], member(azim, peer(i))
        ).wait(),
    )
    relay.wait()


def attention_kernel(same, other, mask, out_same, out_other, rows_all, cols_all, cols_own, allowed, back, keys_sum):
    core = lax.rem(lax.axis_index("azim"), 2)
    sub = lax.broadcasted_iota(jnp.int32, (32, 32), 0)
    lane = lax.broadcasted_iota(jnp.int32, (32, 32), 1)
    key_sector = jnp.where(sub < CHIPS, 2 * sub + core, 2 * (sub - CHIPS) + 1 - core)
    key_hot = jnp.where(lane == key_sector, 1.0, 0.0).astype(BF16)
    by_query = dot_nt(key_hot, mask[...].astype(F32).astype(BF16)).astype(BF16)
    lane = lax.broadcasted_iota(jnp.int32, (32, 1024), 1)
    sub = lax.broadcasted_iota(jnp.int32, (32, 1024), 0)
    query_hot = jnp.where(sub == 2 * (lane >> 6) + core, 1.0, 0.0).astype(BF16)
    full = dot(by_query, query_hot)
    rows_all[0:1024] = same[...]
    rows_all[1024:2048] = other[...]
    own_t = same[...].astype(F32).T.astype(BF16)
    cols_all[:, 0:1024] = own_t
    cols_all[:, 1024:2048] = other[...].astype(F32).T.astype(BF16)
    for t in range(1024 // TILE):
        cols_own[t] = own_t[:, t * TILE : (t + 1) * TILE]
        allowed[t] = full[:, t * TILE : (t + 1) * TILE]
    keys_sum[...] = jnp.zeros_like(keys_sum)

    def tile(t, carry):
        cols = cols_own[t]
        rows = same[pl.ds(pl.multiple_of(t * TILE, TILE), TILE), :]
        keep = allowed[t][:, None, :]
        blank = jnp.zeros((96, TILE), BF16)
        score = dot(rows_all[...], jnp.concatenate([cols[32:64], blank], axis=0))
        score = score.reshape(32, COLS, TILE) * SCALE
        score = jnp.where(keep > 0.5, score, MASKED)
        peak = jnp.max(jnp.max(score, axis=0), axis=0, keepdims=True)
        weight = jnp.exp(score - peak[None])
        total = jnp.sum(jnp.sum(weight, axis=0), axis=0, keepdims=True)
        weight = weight * (keep * (1.0 / total)[None])
        probs = weight.reshape(2048, TILE).astype(BF16)
        attended = dot(cols_all[96:128, :], probs).astype(BF16)
        grad_att = cols[64:96]
        delta = jnp.sum(grad_att.astype(F32) * attended.astype(F32), axis=0, keepdims=True)
        grad_prob = dot(rows_all[...], jnp.concatenate([blank, grad_att], axis=0))
        grad_score = weight * (grad_prob.reshape(32, COLS, TILE) - delta[None])
        grad_score = grad_score.reshape(2048, TILE).astype(BF16)
        grad_query = dot(cols_all[0:32, :], grad_score) * SCALE
        place_at = lax.broadcasted_iota(jnp.int32, (TILE, 128), 1) >> 5
        zero = jnp.zeros((TILE, 128), BF16)
        keys_sum[...] += dot(grad_score, jnp.where(place_at == 1, rows, zero)) * SCALE + dot(
            probs, jnp.where(place_at == 2, rows, zero)
        )
        joined = jnp.concatenate(
            [grad_query, jnp.zeros((64, TILE), F32), attended.astype(F32)], axis=0
        )
        back[pl.ds(pl.multiple_of(t * TILE, TILE), TILE), :] = joined.T
        return carry

    lax.fori_loop(0, 1024 // TILE, tile, 0)
    out_same[...] = (keys_sum[0:1024] + back[...]).astype(BF16)
    out_other[...] = keys_sum[1024:2048].astype(BF16)


def return_kernel(out_same, out_other, from_same, from_other, send, recv, send_o, recv_o, own_sem):
    azim, beam, sweep = place()
    chip = lax.div(azim, 2)
    core = lax.rem(azim, 2)
    target = lambda i: lax.rem(chip + i, CHIPS)
    like = lambda q: (2 * q + core, beam, sweep)
    unlike = lambda q: (2 * q + 1 - core, beam, sweep)
    greet(
        [
            (1, CHIPS, lambda i: like(target(i))),
            (0, CHIPS, lambda i: unlike(target(i))),
        ]
    )
    keep = pltpu.make_async_copy(out_same.at[chip], from_same.at[chip], own_sem)
    keep.start()
    each(
        1,
        CHIPS,
        lambda i: remote(
            out_same.at[target(i)],
            from_same.at[chip],
            send.at[target(i)],
            recv.at[chip],
            like(target(i)),
        ).start(),
    )
    each(
        0,
        CHIPS,
        lambda i: remote(
            out_other.at[target(i)],
            from_other.at[chip],
            send_o.at[target(i)],
            recv_o.at[chip],
            unlike(target(i)),
        ).start(),
    )
    keep.wait()
    each(
        1,
        CHIPS,
        lambda i: remote(
            out_same.at[target(i)],
            from_same.at[target(i)],
            send.at[target(i)],
            recv.at[target(i)],
            like(target(i)),
        ).wait(),
    )
    each(
        0,
        CHIPS,
        lambda i: remote(
            out_other.at[target(i)],
            from_other.at[target(i)],
            send_o.at[target(i)],
            recv_o.at[target(i)],
            unlike(target(i)),
        ).wait(),
    )


def collect_kernel(from_same, from_other, grad, w_query, w_key, w_value, feat_grad, att_out, blocks):
    summed = []
    for b in (0, 1):
        heads = [
            (from_same[b * HEADS + h].astype(F32) + from_other[b * HEADS + h].astype(F32)).astype(BF16)
            for h in range(HEADS)
        ]
        summed.append(jnp.concatenate(heads, axis=1))
    packed = jnp.concatenate(summed, axis=0)
    order = regroup()
    wide = dot_nt(packed, order).astype(BF16)
    grad_f = grad[...]
    feat_grad[...] = (
        grad_f
        + dot_nt(wide[:, 0:256], w_query[...])
        + dot_nt(wide[:, 256:512], w_key[...])
        + dot_nt(wide[:, 512:768], w_value[...])
    ).astype(BF16)
    att_out[...] = wide[:, 768:1024]
    last = dot(grad_f.astype(BF16), order[768:1024, :])
    group = (lax.broadcasted_iota(jnp.int32, (2 * COLS, 1024), 1) >> 5) & 3
    merged = jnp.where(group == 3, last, packed.astype(F32)).astype(BF16)
    for h in range(HEADS):
        blocks[h] = merged[:, h * 128 : (h + 1) * 128]


def share_kernel(att, blocks, att_all, block_all, send, recv, send_b, recv_b):
    azim, beam, sweep = place()
    me = beam * SWEEPS + sweep
    peer = lambda i: lax.rem(me + i, GROUP)
    greet([(1, GROUP, lambda i: member(azim, peer(i)))])
    each(
        1,
        GROUP,
        lambda i: remote(
            att, att_all.at[me], send.at[peer(i)], recv.at[me], member(azim, peer(i))
        ).start(),
    )
    each(
        1,
        GROUP,
        lambda i: remote(
            blocks.at[peer(i)],
            block_all.at[me],
            send_b.at[peer(i)],
            recv_b.at[me],
            member(azim, peer(i)),
        ).start(),
    )
    att_all[pl.ds(me, 1)] = att[...][None]
    block_all[pl.ds(me, 1)] = blocks[pl.ds(me, 1)]
    each(
        1,
        GROUP,
        lambda i: remote(
            att, att_all.at[peer(i)], send.at[peer(i)], recv.at[peer(i)], member(azim, peer(i))
        ).wait(),
    )
    each(
        1,
        GROUP,
        lambda i: remote(
            blocks.at[peer(i)],
            block_all.at[peer(i)],
            send_b.at[peer(i)],
            recv_b.at[peer(i)],
            member(azim, peer(i)),
        ).wait(),
    )


def weight_kernel(cot_all, low, high, feat_all, att_all, block_all, w_out, part, taps):
    _, beam, sweep = place()
    me = beam * SWEEPS + sweep
    row = lax.broadcasted_iota(jnp.int32, (256, 128), 0)
    col = lax.broadcasted_iota(jnp.int32, (256, 128), 1)
    pick = jnp.where(row == me * HEAD + (col & 31), 1.0, 0.0).astype(BF16)
    own = dot(cot_all[...].reshape(1024, 256), pick)
    own_low = dot(low[...], pick)
    own_high = dot(high[...], pick)
    moved = []
    for n in range(16):
        moved.append(
            shifted(
                own[n * COLS : (n + 1) * COLS], own_low[n : n + 1], own_high[n : n + 1]
            )
        )
    lane = lax.broadcasted_iota(jnp.int32, (COLS, 128), 1) >> 5
    zero = jnp.zeros((COLS, 128), F32)

    def find(n, tap):
        if tap >= TAPS:
            return zero
        i, j, k = tap // 9, tap // 3 % 3 - 1, tap % 3 - 1
        s = (n // 2) % SWEEPS - j
        b = (n // 2) // SWEEPS * 2 + n % 2 - k
        if not (0 <= s < SWEEPS and 0 <= b < 4):
            return zero
        return moved[(b // 2 * SWEEPS + s) * 2 + b % 2][i]

    for g in range(7):
        for n in range(16):
            value = find(n, 4 * g)
            for r in (1, 2, 3):
                value = jnp.where(lane == r, find(n, 4 * g + r), value)
            taps[n * COLS : (n + 1) * COLS, g * 128 : (g + 1) * 128] = value.astype(BF16)
    feats = feat_all[...].reshape(1024, 256)
    atts = att_all[...].reshape(1024, 256)
    layer = (feats.astype(F32) + dot(atts, w_out[...])).astype(BF16)
    blocks = block_all[...].reshape(1024, 128)
    first = dot(feats.astype(F32).T.astype(BF16), blocks)
    fourth = dot(atts.astype(F32).T.astype(BF16), blocks)
    col = lax.broadcasted_iota(jnp.int32, (256, 128), 1) >> 5
    part[:, :, 0:128] = jnp.where(col == 3, fourth, first).reshape(RING, 8, 128)
    part[:, :, 128:1024] = dot(layer.astype(F32).T.astype(BF16), taps[...]).reshape(RING, 8, 896)


def reduce_kernel(part, total, landed, send, recv):
    azim, beam, sweep = place()
    target = lambda i: lax.rem(azim + i, RING)
    device = lambda q: (q, beam, sweep)
    greet([(1, RING, lambda i: device(target(i)))])
    each(
        1,
        RING,
        lambda i: remote(
            part.at[target(i)], landed.at[azim], send.at[target(i)], recv.at[azim], device(target(i))
        ).start(),
    )
    total[...] = part[azim].astype(F32)

    def add(i):
        remote(
            part.at[target(i)],
            landed.at[target(i)],
            send.at[target(i)],
            recv.at[target(i)],
            device(target(i)),
        ).wait()
        total[...] += landed[target(i)].astype(F32)

    each(1, RING, add)


def shape(dims, kind=BF16):
    return jax.ShapeDtypeStruct(dims, kind)


def call(kernel, inputs, outputs, scratch, collective=None):
    remote_call = collective is not None
    return pl.pallas_call(
        kernel,
        out_shape=outputs,
        in_specs=[VMEM] * len(inputs),
        out_specs=jax.tree.map(lambda _: VMEM, outputs),
        scratch_shapes=scratch,
        compiler_params=pltpu.CompilerParams(
            collective_id=collective,
            has_side_effects=remote_call,
            vmem_limit_bytes=60 * 1024 * 1024,
        ),
    )(*inputs)


def dma(*dims):
    return pltpu.SemaphoreType.DMA(dims)


def per_device(features, cotangent, w_query, w_key, w_value, w_out, w_conv, sector_mask):
    feat = features.reshape(COLS, 2, 256).transpose(1, 0, 2)
    cot = cotangent.reshape(COLS, 2, 256).transpose(1, 0, 2)
    edges = jnp.stack([cotangent[0, 0], cotangent[COLS - 1, 0]])
    conv = w_conv.transpose(1, 0, 2)
    feat = feat.reshape(2 * COLS, 256)
    cot_all, low, high = call(
        halo_kernel,
        (cot, edges),
        (shape((GROUP, 2, COLS, 256)), shape((GROUP, 2, 256)), shape((GROUP, 2, 256))),
        [dma(GROUP) for _ in range(6)],
        1,
    )
    grad, pack = call(
        project_kernel,
        (cot_all, low, high, feat, w_query, w_key, w_value, w_out, conv),
        (shape((2 * COLS, 256), F32), shape((CHIPS, COLS, 128))),
        [],
    )
    same, other, feat_all = call(
        spread_kernel,
        (pack, feat),
        (shape((CHIPS, COLS, 128)), shape((CHIPS, COLS, 128)), shape((GROUP, 2 * COLS, 256))),
        [dma(CHIPS), dma(CHIPS), dma(GROUP), dma(GROUP), pltpu.SemaphoreType.DMA, dma(2)],
        2,
    )
    out_same, out_other = call(
        attention_kernel,
        (same.reshape(1024, 128), other.reshape(1024, 128), sector_mask),
        (shape((1024, 128)), shape((1024, 128))),
        [
            pltpu.VMEM((2048, 128), BF16),
            pltpu.VMEM((128, 2048), BF16),
            pltpu.VMEM((1024 // TILE, 128, TILE), BF16),
            pltpu.VMEM((1024 // TILE, 32, TILE), F32),
            pltpu.VMEM((1024, 128), F32),
            pltpu.VMEM((2048, 128), F32),
        ],
    )
    from_same, from_other = call(
        return_kernel,
        (out_same.reshape(CHIPS, COLS, 128), out_other.reshape(CHIPS, COLS, 128)),
        (shape((CHIPS, COLS, 128)), shape((CHIPS, COLS, 128))),
        [dma(CHIPS), dma(CHIPS), dma(CHIPS), dma(CHIPS), pltpu.SemaphoreType.DMA],
        3,
    )
    feat_grad, att, blocks = call(
        collect_kernel,
        (from_same, from_other, grad, w_query, w_key, w_value),
        (shape((2 * COLS, 256)), shape((2 * COLS, 256)), shape((HEADS, 2 * COLS, 128))),
        [],
    )
    att_all, block_all = call(
        share_kernel,
        (att, blocks),
        (shape((GROUP, 2 * COLS, 256)), shape((GROUP, 2 * COLS, 128))),
        [dma(GROUP) for _ in range(4)],
        4,
    )
    part = call(
        weight_kernel,
        (
            cot_all,
            low.reshape(16, 256),
            high.reshape(16, 256),
            feat_all,
            att_all,
            block_all,
            w_out,
        ),
        shape((RING, 8, 1024), F32),
        [pltpu.VMEM((1024, 896), BF16)],
    )
    total = call(
        reduce_kernel,
        (part.astype(BF16),),
        shape((8, 1024), F32),
        [pltpu.VMEM((RING, 8, 1024), BF16), dma(RING), dma(RING)],
        5,
    )
    weight_grads = total.reshape(8, 32, 32)[:, :31, :]
    features_grad = feat_grad.reshape(2, COLS, 256).transpose(1, 0, 2)[:, None]
    return features_grad, weight_grads


def solution(mesh):
    token = P("azim", "sweep", "beam", None)
    in_specs = (token, token) + (P(),) * 6
    out_specs = (token, P("azim", None, ("beam", "sweep")))
    return jax.shard_map(
        per_device, mesh=mesh, in_specs=in_specs, out_specs=out_specs, check_vma=False
    )
```

```python
import jax
import jax.numpy as jnp
from jax import lax
from jax.experimental import pallas as pl
from jax.experimental.pallas import tpu as pltpu
from jax.sharding import PartitionSpec as P

HEADS = 8
HEAD = 32
COLS = 64
RING = 32
CHIPS = 16
GROUP = 8
SWEEPS = 4
TAPS = 27
TILE = 256
SCALE = HEAD ** (-0.5)
MASKED = -1e30
MESH = pl.DeviceIdType.MESH
VMEM = pl.BlockSpec(memory_space=pltpu.VMEM)
F32 = jnp.float32
BF16 = jnp.bfloat16


def place():
    return lax.axis_index("azim"), lax.axis_index("beam"), lax.axis_index("sweep")


def member(azim, index):
    return (azim, lax.div(index, SWEEPS), lax.rem(index, SWEEPS))


def remote(src, dst, send, recv, device):
    return pltpu.make_async_remote_copy(
        src_ref=src, dst_ref=dst, send_sem=send, recv_sem=recv, device_id=device, device_id_type=MESH
    )


def each(first, last, action):
    def step(i, carry):
        action(i)
        return carry

    lax.fori_loop(first, last, step, 0)


def shifted(block, low, high):
    rows = lax.broadcasted_iota(jnp.int32, block.shape, 0)
    down = jnp.where(rows == 0, low, pltpu.roll(block, 1, 0))
    up = jnp.where(rows == COLS - 1, high, pltpu.roll(block, COLS - 1, 0))
    return up, block, down


def regroup():
    col = lax.broadcasted_iota(jnp.int32, (1, 1024), 1)
    source = ((col >> 5) & 3) * 256 + (col >> 7) * 32 + (col & 31)
    row = lax.broadcasted_iota(jnp.int32, (1024, 1024), 0)
    return jnp.where(row == source, 1.0, 0.0).astype(BF16)


def dot(left, right):
    return jnp.dot(left, right, preferred_element_type=F32)


def dot_nt(left, right):
    return lax.dot_general(left, right, (((1,), (1,)), ((), ())), preferred_element_type=F32)


def split_beams(block):
    wide = block[...].astype(F32)
    return jnp.concatenate([wide[:, 0, :], wide[:, 1, :]], axis=0)


class Route:
    def __init__(self):
        self.azim, self.beam, self.sweep = place()
        self.me = self.beam * SWEEPS + self.sweep
        self.chip = lax.div(self.azim, 2)
        self.core = lax.rem(self.azim, 2)
        self.sibling = (2 * self.chip + 1 - self.core, self.beam, self.sweep)
        self.after = lax.rem(self.azim + 1, RING)
        self.before = lax.rem(self.azim + RING - 1, RING)

    def ring(self, i):
        return (lax.rem(self.azim + i, RING), self.beam, self.sweep)

    def target(self, i):
        return lax.rem(self.chip + i, CHIPS)

    def like(self, q):
        return (2 * q + self.core, self.beam, self.sweep)

    def peer(self, i):
        return lax.rem(self.me + i, GROUP)

    def mate(self, index):
        return member(self.azim, index)

    def beside(self, d, other):
        beam = 1 - self.beam if other else self.beam
        return (self.azim, beam, lax.rem(self.sweep + d + SWEEPS, SWEEPS))


def greet_all(r):
    barrier = pltpu.get_barrier_semaphore()

    def tell(device):
        pl.semaphore_signal(barrier, inc=1, device_id=device, device_id_type=MESH)

    each(1, RING, lambda i: tell(r.ring(i)))
    each(1, GROUP, lambda i: tell(member(r.after, r.peer(i))))
    each(1, GROUP, lambda i: tell(member(r.before, r.peer(i))))
    each(1, GROUP, lambda i: tell(r.mate(r.peer(i))))
    return barrier, RING - 1 + 3 * (GROUP - 1)


def edge_copies(r, cot, low, high, sems):
    def up(i, slot):
        return remote(cot.at[COLS - 1], low.at[slot], sems.at[0, i], sems.at[1, slot], member(r.after, i))

    def down(i, slot):
        return remote(cot.at[0], high.at[slot], sems.at[2, i], sems.at[3, slot], member(r.before, i))

    return up, down


def near_copies(r, cot_own, near, near_half, sems):
    copies = []
    for slot, d in ((0, 1), (1, -1)):
        copies.append(remote(cot_own, near.at[slot], sems.at[0, slot], sems.at[1, slot], r.beside(d, False)))
    for d in (-1, 0, 1):
        copies.append(
            remote(
                cot_own.at[1 - r.beam],
                near_half.at[1 - d],
                sems.at[0, 3 - d],
                sems.at[1, 3 - d],
                r.beside(d, True),
            )
        )
    return copies


def grad_of_layer(r, own, near, near_half, low, high, conv):
    total = own
    for j in (-1, 0, 1):
        for k in (-1, 0, 1):
            ups, mids, downs = [], [], []
            for mine in (0, 1):
                s_at = r.sweep - j
                inside = (s_at >= 0) & (s_at < SWEEPS)
                if mine - k == -1:
                    inside = inside & (r.beam == 1)
                    block = near_half[1 - j]
                elif mine - k == 2:
                    inside = inside & (r.beam == 0)
                    block = near_half[1 - j]
                elif j == 0:
                    block = own[(mine - k) * COLS : (mine - k + 1) * COLS]
                else:
                    block = near[0 if j == 1 else 1, mine - k]
                s_at = jnp.clip(s_at, 0, SWEEPS - 1)
                index = jnp.clip(r.beam + (mine - k) // 2, 0, 1) * SWEEPS + s_at
                half = (mine - k) % 2
                keep = jnp.where(inside, 1.0, 0.0)
                up, mid, down = shifted(
                    block.astype(F32) * keep,
                    low[index].astype(F32)[half : half + 1] * keep,
                    high[index].astype(F32)[half : half + 1] * keep,
                )
                ups.append(up)
                mids.append(mid)
                downs.append(down)
            for i, rows in ((-1, ups), (0, mids), (1, downs)):
                tap = 9 * (i + 1) + 3 * (j + 1) + (k + 1)
                total += dot_nt(jnp.concatenate(rows, axis=0).astype(BF16), conv[tap])
    return total


def attend(core, same, other, mask, cols_all, cols_own, allowed, back, keys_sum):
    sub = lax.broadcasted_iota(jnp.int32, (32, 32), 0)
    lane = lax.broadcasted_iota(jnp.int32, (32, 32), 1)
    key_sector = jnp.where(sub < CHIPS, 2 * sub + core, 2 * (sub - CHIPS) + 1 - core)
    key_hot = jnp.where(lane == key_sector, 1.0, 0.0).astype(BF16)
    by_query = dot_nt(key_hot, mask[...].astype(F32).astype(BF16)).astype(BF16)
    lane = lax.broadcasted_iota(jnp.int32, (32, 1024), 1)
    sub = lax.broadcasted_iota(jnp.int32, (32, 1024), 0)
    query_hot = jnp.where(sub == 2 * (lane >> 6) + core, 1.0, 0.0).astype(BF16)
    full = dot(by_query, query_hot)
    own = same[...].reshape(1024, 128)
    own_t = own.astype(F32).T.astype(BF16)
    cols_all[:, 0:1024] = own_t
    cols_all[:, 1024:2048] = other[...].reshape(1024, 128).astype(F32).T.astype(BF16)
    for t in range(1024 // TILE):
        cols_own[t] = own_t[:, t * TILE : (t + 1) * TILE]
        allowed[t] = full[:, t * TILE : (t + 1) * TILE]
    keys_sum[...] = jnp.zeros_like(keys_sum)

    def tile(t, carry):
        cols = cols_own[t]
        rows = same[pl.ds(t * (TILE // COLS), TILE // COLS)].reshape(TILE, 128)
        rows_all = jnp.concatenate([same[...], other[...]], axis=0).reshape(2048, 128)
        keep = allowed[t][:, None, :]
        blank = jnp.zeros((96, TILE), BF16)
        score = dot(rows_all, jnp.concatenate([cols[32:64], blank], axis=0))
        score = score.reshape(32, COLS, TILE) * SCALE
        score = jnp.where(keep > 0.5, score, MASKED)
        peak = jnp.max(jnp.max(score, axis=0), axis=0, keepdims=True)
        weight = jnp.exp(score - peak[None])
        total = jnp.sum(jnp.sum(weight, axis=0), axis=0, keepdims=True)
        weight = weight * (keep * (1.0 / total)[None])
        probs = weight.reshape(2048, TILE).astype(BF16)
        attended = dot(cols_all[96:128, :], probs).astype(BF16)
        grad_att = cols[64:96]
        delta = jnp.sum(grad_att.astype(F32) * attended.astype(F32), axis=0, keepdims=True)
        grad_prob = dot(rows_all, jnp.concatenate([blank, grad_att], axis=0))
        grad_score = weight * (grad_prob.reshape(32, COLS, TILE) - delta[None])
        grad_score = grad_score.reshape(2048, TILE).astype(BF16)
        grad_query = dot(cols_all[0:32, :], grad_score) * SCALE
        place_at = lax.broadcasted_iota(jnp.int32, (TILE, 128), 1) >> 5
        zero = jnp.zeros((TILE, 128), BF16)
        keys_sum[...] += (
            dot(grad_score, jnp.where(place_at == 1, rows, zero)) * SCALE
            + dot(probs, jnp.where(place_at == 2, rows, zero))
        ).reshape(2, 1024, 128)
        joined = jnp.concatenate(
            [grad_query, jnp.zeros((64, TILE), F32), attended.astype(F32)], axis=0
        )
        back[pl.ds(pl.multiple_of(t * TILE, TILE), TILE), :] = joined.T
        return carry

    lax.fori_loop(0, 1024 // TILE, tile, 0)


def fill_taps(me, cot_all, low, high, taps):
    row = lax.broadcasted_iota(jnp.int32, (256, 128), 0)
    col = lax.broadcasted_iota(jnp.int32, (256, 128), 1)
    pick = jnp.where(row == me * HEAD + (col & 31), 1.0, 0.0).astype(BF16)
    own = dot(cot_all[...].reshape(1024, 256), pick)

    def flat(ref):
        wide = ref[...].astype(F32)
        return dot(wide.reshape(16, 256).astype(BF16), pick)

    own_low = flat(low)
    own_high = flat(high)
    moved = []
    for n in range(16):
        moved.append(
            shifted(own[n * COLS : (n + 1) * COLS], own_low[n : n + 1], own_high[n : n + 1])
        )
    lane = lax.broadcasted_iota(jnp.int32, (COLS, 128), 1) >> 5
    zero = jnp.zeros((COLS, 128), F32)

    def find(n, tap):
        if tap >= TAPS:
            return zero
        i, j, k = tap // 9, tap // 3 % 3 - 1, tap % 3 - 1
        s = (n // 2) % SWEEPS - j
        b = (n // 2) // SWEEPS * 2 + n % 2 - k
        if not (0 <= s < SWEEPS and 0 <= b < 4):
            return zero
        return moved[(b // 2 * SWEEPS + s) * 2 + b % 2][i]

    for g in range(7):
        for n in range(16):
            value = find(n, 4 * g)
            for r in (1, 2, 3):
                value = jnp.where(lane == r, find(n, 4 * g + r), value)
            taps[n * COLS : (n + 1) * COLS, g * 128 : (g + 1) * 128] = value.astype(BF16)


def whole_kernel(
    features,
    cotangent,
    w_query,
    w_key,
    w_value,
    w_out,
    w_conv,
    mask,
    feat_grad,
    total,
    conv,
    feat,
    cot_own,
    near,
    near_half,
    low,
    high,
    cot_all,
    feat_all,
    order,
    pack,
    same,
    other,
    cols_all,
    cols_own,
    allowed,
    back,
    keys_sum,
    keys_in,
    out_same,
    from_same,
    grad_keep,
    att,
    blocks,
    att_all,
    block_all,
    taps,
    part,
    part_in,
    merged,
    landed,
    conv_sem,
    edge_sem,
    near_sem,
    cot_sem,
    feat_sem,
    pack_sem,
    pair_sem,
    keys_sem,
    back_sem,
    att_sem,
    block_sem,
    part_sem,
    sum_sem,
):
    r = Route()
    load = pltpu.make_async_copy(w_conv, conv, conv_sem)
    load.start()
    barrier, expected = greet_all(r)
    order[...] = regroup()
    feat[...] = split_beams(features).astype(BF16)
    own = split_beams(cotangent)
    cot_own[...] = own.astype(BF16).reshape(2, COLS, 256)
    rows = feat[...]
    queries = dot(rows, w_query[...]).astype(BF16)
    keys = dot(rows, w_key[...]).astype(BF16)
    values = dot(rows, w_value[...]).astype(BF16)
    feat_all[pl.ds(r.me, 1)] = rows[None]
    cot_all[pl.ds(r.me, 1)] = cot_own[...][None]
    pl.semaphore_wait(barrier, expected)

    up, down = edge_copies(r, cotangent, low, high, edge_sem)
    near_all = near_copies(r, cot_own, near, near_half, near_sem)
    each(0, GROUP, lambda i: up(i, r.me).start())
    each(0, GROUP, lambda i: down(i, r.me).start())
    for copy in near_all:
        copy.start()
    load.wait()
    each(0, GROUP, lambda i: up(i, i).wait())
    each(0, GROUP, lambda i: down(i, i).wait())
    for copy in near_all:
        copy.wait()
    grad = grad_of_layer(r, own, near, near_half, low, high, conv)
    grad_keep[...] = grad
    grad_att = dot_nt(grad.astype(BF16), w_out[...]).astype(BF16)
    wide = jnp.concatenate([keys, queries, grad_att, values], axis=1)
    packed = dot(wide, order[...]).astype(BF16)
    for b in (0, 1):
        for h in range(HEADS):
            pack[b * HEADS + h] = packed[b * COLS : (b + 1) * COLS, h * 128 : (h + 1) * 128]

    def head_copy(i, slot):
        return remote(
            pack.at[r.target(i)],
            same.at[slot],
            pack_sem.at[0, r.target(i)],
            pack_sem.at[1, slot],
            r.like(r.target(i)),
        )

    def relay(q):
        return remote(same.at[q], other.at[q], pair_sem.at[0, q], pair_sem.at[1, q], r.sibling)

    def cot_copy(i, slot):
        return remote(
            cot_own, cot_all.at[slot], cot_sem.at[0, r.peer(i)], cot_sem.at[1, slot], r.mate(r.peer(i))
        )

    def feat_copy(i, slot):
        return remote(
            feat, feat_all.at[slot], feat_sem.at[0, r.peer(i)], feat_sem.at[1, slot], r.mate(r.peer(i))
        )

    each(1, CHIPS, lambda i: head_copy(i, r.chip).start())
    keep = pltpu.make_async_copy(pack.at[r.chip], same.at[r.chip], conv_sem)
    keep.start()
    each(1, GROUP, lambda i: cot_copy(i, r.me).start())
    each(1, GROUP, lambda i: feat_copy(i, r.me).start())
    keep.wait()
    relay(r.chip).start()

    def pass_on(i):
        head_copy(i, r.target(i)).wait()
        relay(r.target(i)).start()

    each(1, CHIPS, pass_on)
    each(0, CHIPS, lambda q: relay(q).wait())

    attend(r.core, same, other, mask, cols_all, cols_own, allowed, back, keys_sum)

    swap = remote(keys_sum.at[1], keys_in, keys_sem.at[0], keys_sem.at[1], r.sibling)
    swap.start()
    swap.wait()
    out_same[...] = (keys_sum[0] + back[...] + keys_in[...]).astype(BF16).reshape(CHIPS, COLS, 128)

    def back_copy(i, slot):
        return remote(
            out_same.at[r.target(i)],
            from_same.at[slot],
            back_sem.at[0, r.target(i)],
            back_sem.at[1, slot],
            r.like(r.target(i)),
        )

    each(1, CHIPS, lambda i: back_copy(i, r.chip).start())
    from_same[pl.ds(r.chip, 1)] = out_same[pl.ds(r.chip, 1)]
    each(1, GROUP, lambda i: cot_copy(i, r.peer(i)).wait())
    each(1, GROUP, lambda i: feat_copy(i, r.peer(i)).wait())
    fill_taps(r.me, cot_all, low, high, taps)
    each(1, CHIPS, lambda i: back_copy(i, r.target(i)).wait())

    packed = jnp.concatenate(
        [
            jnp.concatenate([from_same[b * HEADS + h] for h in range(HEADS)], axis=1)
            for b in (0, 1)
        ],
        axis=0,
    )
    grad = grad_keep[...]
    last = dot(grad.astype(BF16), order[768:1024, :])
    group = (lax.broadcasted_iota(jnp.int32, (2 * COLS, 1024), 1) >> 5) & 3
    mixed = jnp.where(group == 3, last, packed.astype(F32)).astype(BF16)
    for h in range(HEADS):
        blocks[h] = mixed[:, h * 128 : (h + 1) * 128]
    wide = dot_nt(packed, order[...]).astype(BF16)
    att[...] = wide[:, 768:1024]

    def att_copy(i, slot):
        return remote(
            att, att_all.at[slot], att_sem.at[0, r.peer(i)], att_sem.at[1, slot], r.mate(r.peer(i))
        )

    def block_copy(i, slot):
        return remote(
            blocks.at[r.peer(i)],
            block_all.at[slot],
            block_sem.at[0, r.peer(i)],
            block_sem.at[1, slot],
            r.mate(r.peer(i)),
        )

    each(1, GROUP, lambda i: att_copy(i, r.me).start())
    each(1, GROUP, lambda i: block_copy(i, r.me).start())
    att_all[pl.ds(r.me, 1)] = wide[:, 768:1024][None]
    block_all[pl.ds(r.me, 1)] = blocks[pl.ds(r.me, 1)]
    feat_grad[...] = (
        grad
        + dot_nt(wide[:, 0:256], w_query[...])
        + dot_nt(wide[:, 256:512], w_key[...])
        + dot_nt(wide[:, 512:768], w_value[...])
    ).astype(BF16)
    feats = feat_all[...].reshape(1024, 256)
    feats_t = feats.astype(F32).T.astype(BF16)
    each(1, GROUP, lambda i: att_copy(i, r.peer(i)).wait())
    each(1, GROUP, lambda i: block_copy(i, r.peer(i)).wait())

    atts = att_all[...].reshape(1024, 256)
    layer = feats.astype(F32) + dot(atts, w_out[...])
    shares = block_all[...].reshape(1024, 128)
    first = dot(feats_t, shares)
    fourth = dot(atts.astype(F32).T.astype(BF16), shares)
    col = lax.broadcasted_iota(jnp.int32, (256, 128), 1) >> 5
    first = jnp.where(col == 3, fourth, first).reshape(CHIPS, 2, 8, 128)
    rest = dot(layer.T.astype(BF16), taps[...]).reshape(CHIPS, 2, 8, 896)
    for c in (0, 1):
        part[c, :, :, 0:128] = first[:, c]
        part[c, :, :, 128:1024] = rest[:, c]

    pair = remote(part.at[1 - r.core], part_in, part_sem.at[0], part_sem.at[1], r.sibling)
    pair.start()
    pair.wait()
    merged[...] = (part[r.core] + part_in[...]).astype(BF16)

    def sum_copy(i, slot):
        return remote(
            merged.at[r.target(i)],
            landed.at[slot],
            sum_sem.at[0, r.target(i)],
            sum_sem.at[1, slot],
            r.like(r.target(i)),
        )

    each(1, CHIPS, lambda i: sum_copy(i, r.chip).start())
    total[...] = merged[r.chip].astype(F32)

    def add(i):
        sum_copy(i, r.target(i)).wait()
        total[...] += landed[r.target(i)].astype(F32)

    each(1, CHIPS, add)


def shape(dims, kind=BF16):
    return jax.ShapeDtypeStruct(dims, kind)


def dma(*dims):
    return pltpu.SemaphoreType.DMA(dims)


def per_device(features, cotangent, w_query, w_key, w_value, w_out, w_conv, sector_mask):
    anywhere = pl.BlockSpec(memory_space=pl.ANY)
    vmem = pltpu.VMEM
    heads = (CHIPS, COLS, 128)
    feat_grad, total = pl.pallas_call(
        whole_kernel,
        out_shape=(shape((2 * COLS, 256)), shape((8, 1024), F32)),
        in_specs=[VMEM] * 6 + [anywhere, VMEM],
        out_specs=(VMEM, VMEM),
        scratch_shapes=[
            vmem((TAPS, 256, 256), BF16),
            vmem((2 * COLS, 256), BF16),
            vmem((2, COLS, 256), BF16),
            vmem((2, 2, COLS, 256), BF16),
            vmem((3, COLS, 256), BF16),
            vmem((GROUP, 2, 256), BF16),
            vmem((GROUP, 2, 256), BF16),
            vmem((GROUP, 2, COLS, 256), BF16),
            vmem((GROUP, 2 * COLS, 256), BF16),
            vmem((1024, 1024), BF16),
            vmem(heads, BF16),
            vmem(heads, BF16),
            vmem(heads, BF16),
            vmem((128, 2048), BF16),
            vmem((1024 // TILE, 128, TILE), BF16),
            vmem((1024 // TILE, 32, TILE), F32),
            vmem((1024, 128), F32),
            vmem((2, 1024, 128), F32),
            vmem((1024, 128), F32),
            vmem(heads, BF16),
            vmem(heads, BF16),
            vmem((2 * COLS, 256), F32),
            vmem((2 * COLS, 256), BF16),
            vmem((HEADS, 2 * COLS, 128), BF16),
            vmem((GROUP, 2 * COLS, 256), BF16),
            vmem((GROUP, 2 * COLS, 128), BF16),
            vmem((1024, 896), BF16),
            vmem((2, CHIPS, 8, 1024), F32),
            vmem((CHIPS, 8, 1024), F32),
            vmem((CHIPS, 8, 1024), BF16),
            vmem((CHIPS, 8, 1024), BF16),
            pltpu.SemaphoreType.DMA,
            dma(4, GROUP),
            dma(2, 5),
            dma(2, GROUP),
            dma(2, GROUP),
            dma(2, CHIPS),
            dma(2, CHIPS),
            dma(2),
            dma(2, CHIPS),
            dma(2, GROUP),
            dma(2, GROUP),
            dma(2),
            dma(2, CHIPS),
        ],
        compiler_params=pltpu.CompilerParams(
            collective_id=1, has_side_effects=True, vmem_limit_bytes=62 * 1024 * 1024
        ),
    )(
        features.reshape(COLS, 2, 256),
        cotangent.reshape(COLS, 2, 256),
        w_query,
        w_key,
        w_value,
        w_out,
        w_conv.transpose(1, 0, 2),
        sector_mask,
    )
    weight_grads = total.reshape(8, 32, 32)[:, :31, :]
    features_grad = feat_grad.reshape(2, COLS, 256).transpose(1, 0, 2)[:, None]
    return features_grad, weight_grads


def solution(mesh):
    token = P("azim", "sweep", "beam", None)
    in_specs = (token, token) + (P(),) * 6
    out_specs = (token, P("azim", None, ("beam", "sweep")))
    return jax.shard_map(
        per_device, mesh=mesh, in_specs=in_specs, out_specs=out_specs, check_vma=False
    )
```
